32 devices in a mesh: groups: 2 (over y), image: 16 (over z, x, core).
Axes of the slice: x: 2, y: 2, z: 4, core: 2. Of those that a mesh axis runs over, the one named last changes fastest.
Arguments:
- vision: bfloat16 [32, 256, 8192], P(('groups', 'image')), parts along dimension 0, may hold values from -6 to 6
- queries: bfloat16 [32, 4096], P(('groups', 'image')), parts along dimension 0, may hold values from -480 to 480
- text_request: int32 [32], P(('groups', 'image')), parts along dimension 0, may hold values from 0 to 7, never falling along the last dimension, each value on 1 to 4 neighbouring positions
- key_weight: bfloat16 [8192, 512], P('image'), may hold values from -0.0625 to 0.0625
- value_weight: bfloat16 [8192, 512], P('image'), may hold values from -0.0625 to 0.0625
- key_gain: float32 [128], replicated, may hold values from 0.25 to 1.75
- down_pages: bfloat16 [8192, 256], P('image'), may hold values from -0.0625 to 0.0625
- up_pages: bfloat16 [16, 16, 512], replicated, may hold values from -1.5 to 1.5
- image_request: int32 [32, 1], P(('groups', 'image')), parts along dimension 0, may hold values from 0 to 7
- image_tiles: int32 [32], P(('groups', 'image')), parts along dimension 0, may hold values from 1 to 4
- request_tenant: int32 [16], P('groups'), parts along dimension 0, may hold values from 0 to 15
- tenant_page: int32 [16], replicated, may hold values from 0 to 15, each once
Outputs:
- attended: bfloat16 [32, 4096], P(('groups', 'image')), parts along dimension 0
The draws below stay inside these ranges and needn't reach their ends.
There are 2 independent parts, one for each index of `groups`. The reference program is written for one: setup_inputs(seed, part) draws one part's arguments, and reference() takes and returns one part's arrays. A program takes and returns all parts, laid end to end along the dimension named above; an argument that names none is the same for every part. Nothing has to cross between parts.
Inputs may be any that keep to these rules, and one draw needn't show every extreme that they name: `text_request`: each request's text tokens are consecutive, 1 to 4 of them, requests in increasing order. `image_request`: every request owns at least one image. `tenant_page`: each page once.
All inputs are finite; a program needn't handle non-finite values.
Results may differ from the reference program's by a relative error of at most 0.012.
The reference program's roundings to bfloat16 on the way (of `lowrank`, `value_block`, `key_block` and `weights`) count: a program that leaves them out, or rounds other values in their place, can miss the bound.
Values may be sent and summed in bfloat16 or wider, within the bound.
A program may use at most 128 MiB of HBM per device.

```python
import math
import jax
import jax.numpy as jnp
import numpy as np
from jax import lax

D = 8192
HEAD = 128
Q_HEADS = 32
KV_HEADS = 4
RANK = 16
TENANTS = 16
TILES = 4
V_DEV = 256
TXT_DEV = 1
IMAGES = 16
REQUESTS = 8
TEXT = 16
TILE_TOK = 64


def draw_queries(key, part):
    normal_part = 3.0 * jax.random.truncated_normal(key, -4.0, 4.0, (TEXT, Q_HEADS * HEAD), jnp.float32)
    return normal_part.astype(jnp.bfloat16)


def plant(entries, own_key, low, top_value):
    index_at = [jax.random.randint(jax.random.fold_in(own_key, axis), (), 0, length) for axis, length in enumerate(entries.shape)]
    widest = entries.shape.index(max(entries.shape))
    beside = index_at[:widest] + [(index_at[widest] + 1) % entries.shape[widest]] + index_at[widest + 1:]
    return entries.at[tuple(index_at)].set(low).at[tuple(beside)].set(top_value)


def steps_of(own_key, dims, pieces, smallest, top_value):
    level, own = 1.0, jax.random.fold_in(own_key, 6)
    for axis_at, blocks in pieces:
        draws = jnp.exp(jax.random.uniform(jax.random.fold_in(own, axis_at), (blocks,), jnp.float32, smallest / len(pieces), top_value / len(pieces)))
        level = level * jnp.repeat(draws, dims[axis_at] // blocks).reshape([-1 if axis == axis_at else 1 for axis in range(len(dims))])
    return level


def choose_distinct(own_key, rows, number_of, top, lift):
    order = jax.random.permutation(jax.random.fold_in(own_key, 1), number_of)
    favour = order
    for power in range(3):
        favour = favour * favour // number_of
    favour = favour * lift // number_of
    tickets = jax.random.randint(jax.random.fold_in(own_key, 2), (rows, number_of), 0, 4096) + favour
    holders = jax.random.permutation(jax.random.fold_in(own_key, 3), rows)[jnp.arange(number_of) % rows]
    tickets = jnp.where(jnp.arange(rows)[:, None] == holders[None, :], 1 << 14, tickets)
    priority = tickets * number_of + jnp.arange(number_of)
    return lax.top_k(priority.astype(jnp.int32), top)[1].astype(jnp.int32)


def length_profile(count, total, reach, lean):
    weights = [(1 << 20) // math.isqrt(grade ** lean) + 1 for grade in range(2, count + 1)]
    surplus, counts = total - reach - (count - 1), [1] * (count - 1)
    while surplus > 0:
        candidates = [i for i in range(count - 1) if counts[i] < reach]
        whole, budget = sum([weights[i] for i in candidates]), surplus
        for i in candidates:
            more = min(reach - counts[i], max(1, budget * weights[i] // whole), surplus)
            counts[i] = counts[i] + more
            surplus = surplus - more
    return np.array([reach] + counts)


def ragged(stream_key, count, total, limit, lean):
    if count == 2:
        one = jax.random.randint(stream_key, (), max(1, total - limit), min(limit, total - 1) + 1)
        return jnp.stack([one, total - one])
    sizes = jnp.asarray(length_profile(count, total, limit, lean), jnp.int32)
    pairs = (count - 1) // 2
    donor, taker = sizes[1:1 + 2 * pairs:2], sizes[2:2 + 2 * pairs:2]
    room = jnp.minimum(donor - 1, limit - taker)
    shifted = jax.random.randint(jax.random.fold_in(stream_key, 1), (pairs,), 0, 1 << 20) % (room + 1)
    sizes = sizes.at[1:1 + 2 * pairs:2].set(donor - shifted).at[2:2 + 2 * pairs:2].set(taker + shifted)
    return sizes[jax.random.permutation(jax.random.fold_in(stream_key, 2), count)]


def bell_draw(own_key, extent, width, bound, cuts=(), kind=jnp.bfloat16):
    values = jax.random.normal(own_key, extent, jnp.float32) * width
    if len(cuts) > 0:
        values = steps_of(own_key, extent, cuts, -0.22, 0.18) * values
    return jnp.clip(values, min=-bound, max=bound).astype(kind)


def setup_inputs(seed: int = 0, part: int = 0) -> dict:
    key_of = jax.random.split(jax.random.key(seed), 13)
    own_keys = jax.random.split(jax.random.fold_in(key_of[12], part), 13)
    vision = bell_draw(own_keys[0], (IMAGES, V_DEV, D), 1.0, 6.0, ((0, 16),))
    queries = draw_queries(jax.random.fold_in(jax.random.fold_in(key_of[12], part), 71), part)
    text_request = jnp.searchsorted(jnp.cumsum(ragged(own_keys[2], REQUESTS, TEXT, 4 * TXT_DEV, 2)), jnp.arange(TEXT), side="right").astype(jnp.int32)
    key_weight = bell_draw(key_of[3], (D, KV_HEADS * HEAD), D ** -0.5, 0.0625, ((0, 16),))
    value_weight = bell_draw(key_of[4], (D, KV_HEADS * HEAD), D ** -0.5, 0.0625, ((0, 16),))
    key_gain = jnp.clip(1.0 + 0.15 * jax.random.normal(key_of[5], (HEAD,), jnp.float32), 0.25, 1.75)
    down_pages = bell_draw(key_of[6], (D, TENANTS * RANK), D ** -0.5, 0.0625, ((0, 16),))
    up_pages = bell_draw(key_of[7], (TENANTS, RANK, KV_HEADS * HEAD), RANK ** -0.5, 1.5)
    image_request = choose_distinct(own_keys[8], IMAGES, REQUESTS, 1, 2048)
    image_tiles = plant(jax.random.randint(own_keys[9], (IMAGES,), 1, TILES + 1), jax.random.fold_in(own_keys[9], 1), 1, TILES).astype(jnp.int32)
    request_tenant = plant(jax.random.randint(own_keys[10], (REQUESTS,), 0, TENANTS), jax.random.fold_in(own_keys[10], 1), 0, TENANTS - 1).astype(jnp.int32)
    tenant_page = jax.random.permutation(key_of[11], TENANTS).astype(jnp.int32)
    return dict(vision=vision, queries=queries, text_request=text_request, key_weight=key_weight, value_weight=value_weight, key_gain=key_gain, down_pages=down_pages, up_pages=up_pages, image_request=image_request, image_tiles=image_tiles, request_tenant=request_tenant, tenant_page=tenant_page)


epsilon = 1e-05
masked_score = -1e+30

def project_image(image_tokens, key_weight, value_weight, down_factor, up_factor, key_gain):
    key_raw = jnp.dot(image_tokens, key_weight, preferred_element_type=jnp.float32)
    value_raw = jnp.dot(image_tokens, value_weight, preferred_element_type=jnp.float32)
    lowrank = jnp.dot(image_tokens, down_factor, preferred_element_type=jnp.float32).astype(jnp.bfloat16)
    value_block = (value_raw + jnp.dot(lowrank, up_factor, preferred_element_type=jnp.float32)).astype(jnp.bfloat16)
    key_heads = key_raw.reshape(V_DEV, KV_HEADS, HEAD)
    inverse_rms = lax.rsqrt(lax.optimization_barrier(jnp.mean(key_heads * key_heads, axis=-1, keepdims=True)) + epsilon)
    key_block = (key_heads * inverse_rms * key_gain).reshape(V_DEV, KV_HEADS * HEAD).astype(jnp.bfloat16)
    return (key_block, value_block)

def usable_mask(text_request, owner_id, tile_count):
    positions = jnp.arange(V_DEV, dtype=jnp.int32)
    return (text_request[:, None] == owner_id) & (positions[None, :] < tile_count * TILE_TOK)

def score_block(query_heads, key_block, usable):
    key_heads = key_block.astype(jnp.float32).reshape(V_DEV, KV_HEADS, HEAD)
    scores = jnp.einsum('tkgd,vkd->tkgv', query_heads, key_heads) * HEAD ** (-0.5)
    return jnp.where(usable[:, None, None, :], scores, masked_score)

def reference(vision, queries, text_request, key_weight, value_weight, key_gain, down_pages, up_pages, image_request, image_tiles, request_tenant, tenant_page):
    head_group = Q_HEADS // KV_HEADS
    query_heads = queries.astype(jnp.float32).reshape(TEXT, KV_HEADS, head_group, HEAD)

    def first_pass(image_item):
        image_tokens, owner_row, tile_count = image_item
        owner_id = owner_row[0]
        page_id = tenant_page[request_tenant[owner_id]].astype(jnp.int32)
        down_factor = lax.dynamic_slice_in_dim(down_pages, (page_id * RANK).astype(jnp.int32), RANK, 1)
        up_factor = lax.dynamic_index_in_dim(up_pages, page_id, 0, keepdims=False)
        key_block, value_block = project_image(image_tokens, key_weight, value_weight, down_factor, up_factor, key_gain)
        scores = score_block(query_heads, key_block, usable_mask(text_request, owner_id, tile_count))
        return (key_block, value_block, lax.optimization_barrier(jnp.max(scores, axis=-1)))
    key_all, value_all, maxima = lax.map(first_pass, (vision, image_request, image_tiles))
    top_score = lax.optimization_barrier(jnp.max(maxima, axis=0))

    def second_pass(running, image_item):
        key_block, value_block, owner_row, tile_count = image_item
        usable = usable_mask(text_request, owner_row[0], tile_count)
        scores = score_block(query_heads, key_block, usable)
        weights = jnp.where(usable[:, None, None, :], jnp.exp(scores - top_score[..., None]), 0.0).astype(jnp.bfloat16)
        weights = weights.astype(jnp.float32)
        value_heads = value_block.astype(jnp.float32).reshape(V_DEV, KV_HEADS, HEAD)
        numerator = running[0] + jnp.einsum('tkgv,vkd->tkgd', weights, value_heads)
        totals = running[1] + lax.optimization_barrier(jnp.sum(weights, axis=-1))
        return ((numerator, totals), None)
    start_state = (jnp.zeros((TEXT, KV_HEADS, head_group, HEAD), jnp.float32), jnp.zeros((TEXT, KV_HEADS, head_group), jnp.float32))
    final_state, ignored = lax.scan(second_pass, start_state, (key_all, value_all, image_request, image_tiles))
    numerator, totals = final_state
    return (numerator / totals[..., None]).reshape(TEXT, Q_HEADS * HEAD).astype(jnp.bfloat16)
```

```python
import functools

import jax
import jax.numpy as jnp
from jax import lax
from jax.experimental import pallas as pl
from jax.experimental.pallas import tpu as pltpu
from jax.sharding import PartitionSpec as P

HEAD = 128
KV_HEADS = 4
TILES = 4
MESH = pl.DeviceIdType.MESH

epsilon = 1e-05
masked_score = -1e30

LAG_X, LAG_Y, LAG_C = 1, 2, 3


def plane_of(n):
    chips, x_size = n // 2, 1
    while (x_size * 2) ** 3 <= chips:
        x_size *= 2
    return chips // x_size, x_size


def kernel(
    n,
    fy,
    vision_hbm,
    query_hbm,
    text_ref,
    key_hbm,
    value_hbm,
    gain_ref,
    down_ref,
    up_ref,
    owner_ref,
    tiles_ref,
    tenant_ref,
    page_ref,
    out_ref,
    vis,
    wbuf,
    acc,
    qbuf,
    ibuf,
    selb,
    dbuf,
    sbuf,
    pbuf,
    mbuf,
    lbuf,
    low,
    inv,
    obuf,
    rbuf,
    local_sem,
    zs,
    xs,
    ys,
    mps,
    mys,
    plane_r,
    y_r,
    mp_r,
    my_r,
    small_s,
    small_r,
):
    z_size, x_size = plane_of(n)
    rows, width = key_hbm.shape
    rank = up_ref.shape[1]
    keys = vision_hbm.shape[0]
    group_of = qbuf.shape[1] // KV_HEADS
    lanes = n * group_of
    g = lax.axis_index("groups")
    me = lax.axis_index("image")
    c = me % 2
    x = (me // 2) % x_size
    z = me // (2 * x_size)
    part = rows - fy
    p_rows = pl.ds(pl.multiple_of(g * fy, 16), part)
    y_rows = pl.ds(pl.multiple_of(g * part, 16), fy)
    o_rows = pl.ds(pl.multiple_of((1 - g) * part, 16), fy)

    def flat(zz, xx, cc):
        return (zz * x_size + xx) * 2 + cc

    owner = owner_ref[0, 0]
    page = page_ref[tenant_ref[owner]]

    load_vis = pltpu.make_async_copy(vision_hbm, vis, local_sem.at[0])
    load_key = pltpu.make_async_copy(key_hbm, wbuf.at[0, z, x, c], local_sem.at[1])
    load_value = pltpu.make_async_copy(value_hbm, wbuf.at[1, z, x, c], local_sem.at[2])
    load_query = pltpu.make_async_copy(query_hbm, qbuf.at[me], local_sem.at[3])
    load_key.start()
    load_query.start()
    load_value.start()
    load_vis.start()
    ibuf[me] = jnp.where(
        lax.broadcasted_iota(jnp.int32, ibuf.shape[1:], 0) == 0, page, text_ref[0]
    )

    barrier = pltpu.get_barrier_semaphore()

    def greet(d, carry):
        pl.semaphore_signal(barrier, inc=1, device_id=(g, (me + d) % n), device_id_type=MESH)
        return carry

    lax.fori_loop(1, n, greet, 0)
    pl.semaphore_signal(barrier, inc=1, device_id=(1 - g, me), device_id_type=MESH)
    pl.semaphore_wait(barrier, n)

    def small(kind, src_of, dst, d):
        peer = (me + d) % n
        return pltpu.make_async_remote_copy(
            src_ref=src_of(peer),
            dst_ref=dst.at[me],
            send_sem=small_s.at[kind, d],
            recv_sem=small_r.at[kind, me],
            device_id=(g, peer),
            device_id_type=MESH,
        )

    def small_start(kind, src_of, dst):
        def body(d, carry):
            small(kind, src_of, dst, d).start()
            return carry

        lax.fori_loop(1, n, body, 0)

    def small_wait(kind, src_of, dst):
        def body(d, carry):
            source = (me + n - d) % n
            pltpu.make_async_remote_copy(
                src_ref=src_of(me),
                dst_ref=dst.at[source],
                send_sem=small_s.at[kind, d],
                recv_sem=small_r.at[kind, source],
                device_id=(g, source),
                device_id_type=MESH,
            ).wait_recv()
            small(kind, src_of, dst, d).wait_send()
            return carry

        lax.fori_loop(1, n, body, 0)

    def from_own(buffer):
        return lambda peer: buffer.at[me]

    info_src, query_src = from_own(ibuf), from_own(qbuf)
    max_src, total_src = from_own(mbuf), from_own(lbuf)

    def to_peer(buffer):
        return lambda peer: buffer.at[peer]

    sel_src, num_src = to_peer(selb), to_peer(obuf)

    def nearest(k):
        low_side = jnp.minimum(z, z_size - 1 - z)
        both = k <= 2 * low_side
        half = (k + 1) // 2
        rest = k - low_side
        paired = jnp.where(k % 2 == 1, z - half, z + half)
        single = jnp.where(z < z_size - 1 - z, z + rest, z - rest)
        return jnp.where(both, paired, single)

    def move(ph, zz, xx, cc, window, send, recv, device):
        ref = wbuf.at[ph, zz, xx, cc, window]
        return pltpu.make_async_remote_copy(
            src_ref=ref,
            dst_ref=ref,
            send_sem=send,
            recv_sem=recv,
            device_id=device,
            device_id_type=MESH,
        )

    def z_copy(ph, zz, up):
        to = z + 1 if up else z - 1
        return move(
            ph, zz, x, c, p_rows, zs.at[0 if up else 1, ph, zz],
            plane_r.at[ph, zz, x], (g, flat(to, x, c)),
        )

    def x_copy(ph, zz, dx):
        return move(
            ph, zz, x, c, p_rows, xs.at[dx - 1, ph, zz],
            plane_r.at[ph, zz, x], (g, flat(z, (x + dx) % x_size, c)),
        )

    def y_copy(ph, zz, xx):
        return move(
            ph, zz, xx, c, y_rows, ys.at[ph, zz, xx], y_r.at[ph, zz, xx], (1 - g, me)
        )

    def mate_p(ph, zz, xx, cc):
        return move(
            ph, zz, xx, cc, p_rows, mps.at[ph, zz, xx], mp_r.at[ph, zz, xx],
            (g, flat(z, x, 1 - c)),
        )

    def mate_y(ph, zz, xx, cc):
        return move(
            ph, zz, xx, cc, o_rows, mys.at[ph, zz, xx], my_r.at[ph, zz, xx],
            (g, flat(z, x, 1 - c)),
        )

    def plane_wait(ph, zz, xx):
        move(
            ph, zz, xx, c, p_rows, mps.at[ph, zz, xx], plane_r.at[ph, zz, xx],
            (g, flat(z, x, 1 - c)),
        ).wait_recv()

    def y_wait(ph, zz, xx):
        move(
            ph, zz, xx, c, o_rows, mys.at[ph, zz, xx], y_r.at[ph, zz, xx], (1 - g, me)
        ).wait_recv()

    def goes_up(zz):
        return jnp.logical_and(zz <= z, z + 1 < z_size)

    def goes_down(zz):
        return jnp.logical_and(zz >= z, z >= 1)

    def z_stage(ph, k):
        zz = nearest(k)

        @pl.when(k > 0)
        def _():
            plane_wait(ph, zz, x)

        @pl.when(jnp.logical_and(k == 0, ph == 1))
        def _():
            load_value.wait()

        @pl.when(goes_up(zz))
        def _():
            z_copy(ph, zz, True).start()

        @pl.when(goes_down(zz))
        def _():
            z_copy(ph, zz, False).start()

        for dx in range(1, x_size):
            x_copy(ph, zz, dx).start()

        @pl.when(k > 0)
        def _():
            y_copy(ph, zz, x).start()

        mate_p(ph, zz, x, c).start()

    def x_stage(ph, k):
        zz = nearest(k)
        for dx in range(1, x_size):
            xx = (x + x_size - dx) % x_size
            plane_wait(ph, zz, xx)
            y_copy(ph, zz, xx).start()
            mate_p(ph, zz, xx, c).start()

    def y_stage(ph, k):
        zz = nearest(k)
        for dx in range(x_size):
            xx = (x + x_size - dx) % x_size
            if dx == 0:

                @pl.when(k > 0)
                def _():
                    y_wait(ph, zz, xx)

            else:
                y_wait(ph, zz, xx)
            mate_y(ph, zz, xx, c).start()

    def c_stage(ph, k):
        zz = nearest(k)
        for dx in range(x_size):
            xx = (x + x_size - dx) % x_size
            mate_p(ph, zz, xx, 1 - c).wait_recv()
            mate_y(ph, zz, xx, 1 - c).wait_recv()
            start = pl.multiple_of((zz * x_size + xx) * (2 * rows), 128)
            columns = vis[:, pl.ds(start, 2 * rows)]
            block = wbuf[ph, zz, xx].reshape(2 * rows, width)
            acc[ph] += jnp.dot(columns, block, preferred_element_type=jnp.float32)

    def first_small():
        small_wait(0, info_src, ibuf)
        small_wait(1, query_src, qbuf)
        pages = down_ref.shape[1]
        row = lax.broadcasted_iota(jnp.int32, (rank, pages), 0)
        column = lax.broadcasted_iota(jnp.int32, (rank, pages), 1)
        chosen = [
            (column == ibuf[d, 0:1, 0:1] * rank + row).astype(jnp.float32).astype(jnp.bfloat16)
            for d in range(n)
        ]
        picked = lax.dot_general(
            jnp.concatenate(chosen, axis=0),
            down_ref[...],
            (((1,), (1,)), ((), ())),
            preferred_element_type=jnp.float32,
        ).astype(jnp.bfloat16)
        selb[...] = picked.reshape(n, rank, rows)
        dbuf[me] = selb[me]
        small_start(2, sel_src, dbuf)
        load_vis.wait()

    def lowrank():
        small_wait(2, sel_src, dbuf)
        total = jnp.zeros((keys, rank), jnp.float32)
        for p in range(n // 2):
            pair = vis[:, p * 2 * rows : (p + 1) * 2 * rows]
            for half in range(2):
                total += lax.dot_general(
                    pair[:, half * rows : (half + 1) * rows],
                    dbuf[2 * p + half],
                    (((1,), (1,)), ((), ())),
                    preferred_element_type=jnp.float32,
                )
        low[...] = jnp.dot(
            total.astype(jnp.bfloat16), up_ref[page], preferred_element_type=jnp.float32
        )

    def usable():
        lane = lax.broadcasted_iota(jnp.int32, (1, lanes), 1) // group_of
        request = jnp.zeros((1, lanes), jnp.int32)
        for t in range(n):
            request = jnp.where(lane == t, ibuf[t, 1:2, 0:1], request)
        position = lax.broadcasted_iota(jnp.int32, (keys, lanes), 0)
        return jnp.logical_and(
            jnp.broadcast_to(request, (keys, lanes)) == owner,
            position < tiles_ref[0] * (keys // TILES),
        )

    def score():
        mask = usable()
        gain = gain_ref[...]
        for h in range(KV_HEADS):
            head = acc[0, :, h * HEAD : (h + 1) * HEAD]
            scale = lax.rsqrt(jnp.mean(head * head, axis=-1, keepdims=True) + epsilon)
            block = (head * scale * gain).astype(jnp.bfloat16)
            query = qbuf[...].astype(jnp.float32)[:, h * group_of : (h + 1) * group_of, :]
            query = query.reshape(lanes, HEAD).astype(jnp.bfloat16)
            s = lax.dot_general(
                block, query, (((1,), (1,)), ((), ())), preferred_element_type=jnp.float32
            ) * HEAD ** (-0.5)
            s = jnp.where(mask, s, masked_score)
            sbuf[h] = s
            mbuf[me, h : h + 1, :] = jnp.max(s, axis=0, keepdims=True)
        small_start(3, max_src, mbuf)

    def weigh():
        small_wait(3, max_src, mbuf)
        mask = usable()
        top = jnp.max(mbuf[...], axis=0)
        for h in range(KV_HEADS):
            w = jnp.where(mask, jnp.exp(sbuf[h] - top[h : h + 1, :]), 0.0).astype(jnp.bfloat16)
            pbuf[h] = w
            lbuf[me, h : h + 1, :] = jnp.sum(w.astype(jnp.float32), axis=0, keepdims=True)
        small_start(4, total_src, lbuf)

    def divide():
        small_wait(4, total_src, lbuf)
        total = jnp.sum(lbuf[...], axis=0)
        for h in range(KV_HEADS):
            inv[h] = jnp.broadcast_to(total[h : h + 1, :], (HEAD, lanes)).T

    acc[...] = jnp.zeros_like(acc)
    mbuf[me] = jnp.zeros(mbuf.shape[1:], jnp.float32)
    lbuf[me] = jnp.zeros(lbuf.shape[1:], jnp.float32)
    load_query.wait()
    small_start(0, info_src, ibuf)
    small_start(1, query_src, qbuf)
    load_key.wait()

    steps = 2 * z_size
    keys_done = z_size - 1 + LAG_C

    def step(t, carry):
        def at(lag, stage):
            now = t - lag

            @pl.when(jnp.logical_and(now >= 0, now < steps))
            def _():
                stage(now // z_size, now % z_size)

        at(0, z_stage)
        at(LAG_X, x_stage)
        at(LAG_Y, y_stage)

        @pl.when(t == 0)
        def _():
            first_small()

        at(LAG_C, c_stage)

        @pl.when(t == 2)
        def _():
            lowrank()

        @pl.when(t == keys_done)
        def _():
            score()

        @pl.when(t == keys_done + 1)
        def _():
            weigh()

        @pl.when(t == keys_done + 2)
        def _():
            divide()

        return carry

    lax.fori_loop(0, steps + LAG_C, step, 0)

    value_block = (acc[1] + low[...]).astype(jnp.bfloat16)
    for h in range(KV_HEADS):
        numerator = lax.dot_general(
            pbuf[h],
            value_block[:, h * HEAD : (h + 1) * HEAD],
            (((0,), (0,)), ((), ())),
            preferred_element_type=jnp.float32,
        )
        share = numerator / inv[h]
        rbuf[:, h * group_of : (h + 1) * group_of, :] = share.reshape(n, group_of, HEAD)
    obuf[...] = rbuf[...].astype(jnp.bfloat16)
    qbuf[me] = obuf[me]
    small_start(5, num_src, qbuf)

    def drain(i, carry):
        ph, k = i // z_size, i % z_size
        zz = nearest(k)

        @pl.when(goes_up(zz))
        def _():
            z_copy(ph, zz, True).wait_send()

        @pl.when(goes_down(zz))
        def _():
            z_copy(ph, zz, False).wait_send()

        for dx in range(1, x_size):
            x_copy(ph, zz, dx).wait_send()
        for dx in range(x_size):
            xx = (x + x_size - dx) % x_size
            if dx == 0:

                @pl.when(k > 0)
                def _():
                    y_copy(ph, zz, xx).wait_send()

            else:
                y_copy(ph, zz, xx).wait_send()
            mate_p(ph, zz, xx, c).wait_send()
            mate_y(ph, zz, xx, c).wait_send()
        return carry

    lax.fori_loop(0, steps, drain, 0)
    small_wait(5, num_src, qbuf)
    out_ref[...] = jnp.sum(qbuf[...].astype(jnp.float32), axis=0).astype(jnp.bfloat16)


def local(
    n,
    vision,
    queries,
    text_request,
    key_weight,
    value_weight,
    key_gain,
    down_pages,
    up_pages,
    image_request,
    image_tiles,
    request_tenant,
    tenant_page,
):
    z_size, x_size = plane_of(n)
    rows, width = key_weight.shape
    keys, model = vision.shape[1:]
    rank = up_pages.shape[1]
    heads = queries.shape[1] // HEAD
    lanes = n * (heads // KV_HEADS)
    fy = rows * 3 // 8 // 16 * 16
    vmem = pl.BlockSpec(memory_space=pltpu.VMEM)
    hbm = pl.BlockSpec(memory_space=pl.ANY)
    smem = pl.BlockSpec(memory_space=pltpu.SMEM)
    dma = pltpu.SemaphoreType.DMA
    blocks = (2, z_size, x_size)
    attended = pl.pallas_call(
        functools.partial(kernel, n, fy),
        out_shape=jax.ShapeDtypeStruct((heads, HEAD), jnp.bfloat16),
        in_specs=[hbm, hbm, smem, hbm, hbm, vmem, vmem, vmem, smem, smem, smem, smem],
        out_specs=vmem,
        scratch_shapes=[
            pltpu.VMEM((keys, model), jnp.bfloat16),
            pltpu.VMEM((2, z_size, x_size, 2, rows, width), jnp.bfloat16),
            pltpu.VMEM((2, keys, width), jnp.float32),
            pltpu.VMEM((n, heads, HEAD), jnp.bfloat16),
            pltpu.VMEM((n, 8, 128), jnp.int32),
            pltpu.VMEM((n, rank, rows), jnp.bfloat16),
            pltpu.VMEM((n, rank, rows), jnp.bfloat16),
            pltpu.VMEM((KV_HEADS, keys, lanes), jnp.float32),
            pltpu.VMEM((KV_HEADS, keys, lanes), jnp.bfloat16),
            pltpu.VMEM((n, 8, lanes), jnp.float32),
            pltpu.VMEM((n, 8, lanes), jnp.float32),
            pltpu.VMEM((keys, width), jnp.float32),
            pltpu.VMEM((KV_HEADS, lanes, HEAD), jnp.float32),
            pltpu.VMEM((n, heads, HEAD), jnp.bfloat16),
            pltpu.VMEM((n, heads, HEAD), jnp.float32),
            dma((4,)),
            dma((2, 2, z_size)),
            dma((max(x_size - 1, 1), 2, z_size)),
            dma(blocks),
            dma(blocks),
            dma(blocks),
            dma(blocks),
            dma(blocks),
            dma(blocks),
            dma(blocks),
            dma((6, n)),
            dma((6, n)),
        ],
        compiler_params=pltpu.CompilerParams(
            collective_id=0, has_side_effects=True, vmem_limit_bytes=60 * 1024 * 1024
        ),
    )(
        vision[0],
        queries.reshape(heads, HEAD),
        text_request,
        key_weight,
        value_weight,
        key_gain.reshape(1, HEAD),
        down_pages,
        up_pages,
        image_request,
        image_tiles,
        request_tenant,
        tenant_page,
    )
    return attended.reshape(1, heads * HEAD)


def solution(mesh):
    in_specs = (
        P(("groups", "image"), None, None),
        P(("groups", "image"), None),
        P(("groups", "image")),
        P("image", None),
        P("image", None),
        P(),
        P("image", None),
        P(),
        P(("groups", "image"), None),
        P(("groups", "image")),
        P("groups"),
        P(),
    )
    out_specs = P(("groups", "image"), None)
    return jax.shard_map(
        functools.partial(local, mesh.shape["image"]),
        mesh=mesh,
        in_specs=in_specs,
        out_specs=out_specs,
        check_vma=False,
    )
```

```python
import functools

import jax
import jax.numpy as jnp
from jax import lax
from jax.experimental import pallas as pl
from jax.experimental.pallas import tpu as pltpu
from jax.sharding import PartitionSpec as P

HEAD = 128
KV_HEADS = 4
TILES = 4
MESH = pl.DeviceIdType.MESH

epsilon = 1e-05
masked_score = -1e30

LAG_X, LAG_Y, LAG_C = 1, 2, 3
SPLIT = 2


def plane_of(n):
    chips, x_size = n // 2, 1
    while (x_size * 2) ** 3 <= chips:
        x_size *= 2
    return chips // x_size, x_size


def kernel(
    n,
    fy,
    vision_hbm,
    query_hbm,
    text_hbm,
    key_hbm,
    value_hbm,
    gain_hbm,
    down_hbm,
    up_hbm,
    owner_hbm,
    tiles_hbm,
    tenant_hbm,
    page_hbm,
    out_ref,
    gain_ref,
    down_ref,
    up_ref,
    text_ref,
    owner_ref,
    tiles_ref,
    tenant_ref,
    page_ref,
    qrow,
    qrows,
    vis,
    wbuf,
    acc,
    qbuf,
    ibuf,
    selb,
    dbuf,
    sbuf,
    pbuf,
    mbuf,
    lbuf,
    low,
    inv,
    obuf,
    rbuf,
    local_sem,
    zs,
    xs,
    ys,
    mps,
    mys,
    plane_r,
    y_r,
    mp_r,
    my_r,
    small_s,
    small_r,
):
    z_size, x_size = plane_of(n)
    rows, width = key_hbm.shape
    rank = up_hbm.shape[1]
    keys = vision_hbm.shape[0]
    group_of = qbuf.shape[1] // KV_HEADS
    lanes = n * group_of
    g = lax.axis_index("groups")
    me = lax.axis_index("image")
    c = me % 2
    x = (me // 2) % x_size
    z = me // (2 * x_size)
    part = rows - fy
    p_rows = pl.ds(pl.multiple_of(g * fy, 16), part)
    y_rows = pl.ds(pl.multiple_of(g * part, 16), fy)
    o_rows = pl.ds(pl.multiple_of((1 - g) * part, 16), fy)

    def flat(zz, xx, cc):
        return (zz * x_size + xx) * 2 + cc

    phases = 2 * SPLIT
    per = width // SPLIT
    scalars = [
        pltpu.make_async_copy(src, dst, local_sem.at[i])
        for i, (src, dst) in enumerate(
            (
                (text_hbm, text_ref),
                (owner_hbm, owner_ref),
                (tiles_hbm, tiles_ref),
                (tenant_hbm, tenant_ref),
                (page_hbm, page_ref),
                (query_hbm, qrow),
            )
        )
    ]
    loads = [
        pltpu.make_async_copy(
            (key_hbm, value_hbm)[ph // SPLIT].at[:, pl.ds(ph % SPLIT * per, per)],
            wbuf.at[ph, z, x, c],
            local_sem.at[6 + ph],
        )
        for ph in range(phases)
    ]
    later = [
        pltpu.make_async_copy(src, dst, local_sem.at[6 + phases + i])
        for i, (src, dst) in enumerate(
            ((vision_hbm, vis), (gain_hbm, gain_ref), (down_hbm, down_ref), (up_hbm, up_ref))
        )
    ]
    for copy in scalars + loads + later:
        copy.start()

    barrier = pltpu.get_barrier_semaphore()

    def greet(d, carry):
        pl.semaphore_signal(barrier, inc=1, device_id=(g, (me + d) % n), device_id_type=MESH)
        return carry

    lax.fori_loop(1, n, greet, 0)
    pl.semaphore_signal(barrier, inc=1, device_id=(1 - g, me), device_id_type=MESH)
    for copy in scalars:
        copy.wait()
    owner = owner_ref[0, 0]
    page = page_ref[tenant_ref[owner]]
    ibuf[me] = jnp.where(
        lax.broadcasted_iota(jnp.int32, ibuf.shape[1:], 0) == 0, page, text_ref[0]
    )
    for h in range(qrows.shape[0]):
        qrows[h : h + 1, :] = qrow[:, h * HEAD : (h + 1) * HEAD].astype(jnp.float32)
    qbuf[me] = qrows[...].astype(jnp.bfloat16)
    for copy in loads:
        copy.wait()
    pl.semaphore_wait(barrier, n)

    def small(kind, src_of, dst, d):
        peer = (me + d) % n
        return pltpu.make_async_remote_copy(
            src_ref=src_of(peer),
            dst_ref=dst.at[me],
            send_sem=small_s.at[kind, d],
            recv_sem=small_r.at[kind, me],
            device_id=(g, peer),
            device_id_type=MESH,
        )

    def small_start(kind, src_of, dst):
        def body(d, carry):
            small(kind, src_of, dst, d).start()
            return carry

        lax.fori_loop(1, n, body, 0)

    def small_wait(kind, src_of, dst):
        def body(d, carry):
            source = (me + n - d) % n
            pltpu.make_async_remote_copy(
                src_ref=src_of(me),
                dst_ref=dst.at[source],
                send_sem=small_s.at[kind, d],
                recv_sem=small_r.at[kind, source],
                device_id=(g, source),
                device_id_type=MESH,
            ).wait_recv()
            small(kind, src_of, dst, d).wait_send()
            return carry

        lax.fori_loop(1, n, body, 0)

    def from_own(buffer):
        return lambda peer: buffer.at[me]

    info_src, query_src = from_own(ibuf), from_own(qbuf)
    max_src, total_src = from_own(mbuf), from_own(lbuf)

    def to_peer(buffer):
        return lambda peer: buffer.at[peer]

    sel_src, num_src = to_peer(selb), to_peer(obuf)

    def nearest(k):
        low_side = jnp.minimum(z, z_size - 1 - z)
        both = k <= 2 * low_side
        half = (k + 1) // 2
        rest = k - low_side
        paired = jnp.where(k % 2 == 1, z - half, z + half)
        single = jnp.where(z < z_size - 1 - z, z + rest, z - rest)
        return jnp.where(both, paired, single)

    def move(ph, zz, xx, cc, window, send, recv, device):
        ref = wbuf.at[ph, zz, xx, cc, window]
        return pltpu.make_async_remote_copy(
            src_ref=ref,
            dst_ref=ref,
            send_sem=send,
            recv_sem=recv,
            device_id=device,
            device_id_type=MESH,
        )

    def z_copy(ph, zz, up):
        to = z + 1 if up else z - 1
        return move(
            ph, zz, x, c, p_rows, zs.at[0 if up else 1, ph, zz],
            plane_r.at[ph, zz, x], (g, flat(to, x, c)),
        )

    def x_copy(ph, zz, dx):
        return move(
            ph, zz, x, c, p_rows, xs.at[dx - 1, ph, zz],
            plane_r.at[ph, zz, x], (g, flat(z, (x + dx) % x_size, c)),
        )

    def y_copy(ph, zz, xx):
        return move(
            ph, zz, xx, c, y_rows, ys.at[ph, zz, xx], y_r.at[ph, zz, xx], (1 - g, me)
        )

    def mate_p(ph, zz, xx, cc):
        return move(
            ph, zz, xx, cc, p_rows, mps.at[ph, zz, xx], mp_r.at[ph, zz, xx],
            (g, flat(z, x, 1 - c)),
        )

    def mate_y(ph, zz, xx, cc):
        return move(
            ph, zz, xx, cc, o_rows, mys.at[ph, zz, xx], my_r.at[ph, zz, xx],
            (g, flat(z, x, 1 - c)),
        )

    def plane_wait(ph, zz, xx):
        move(
            ph, zz, xx, c, p_rows, mps.at[ph, zz, xx], plane_r.at[ph, zz, xx],
            (g, flat(z, x, 1 - c)),
        ).wait_recv()

    def y_wait(ph, zz, xx):
        move(
            ph, zz, xx, c, o_rows, mys.at[ph, zz, xx], y_r.at[ph, zz, xx], (1 - g, me)
        ).wait_recv()

    def goes_up(zz):
        return jnp.logical_and(zz <= z, z + 1 < z_size)

    def goes_down(zz):
        return jnp.logical_and(zz >= z, z >= 1)

    def z_stage(ph, k):
        zz = nearest(k)

        @pl.when(k > 0)
        def _():
            plane_wait(ph, zz, x)

        @pl.when(goes_up(zz))
        def _():
            z_copy(ph, zz, True).start()

        @pl.when(goes_down(zz))
        def _():
            z_copy(ph, zz, False).start()

        for dx in range(1, x_size):
            x_copy(ph, zz, dx).start()

        @pl.when(k > 0)
        def _():
            y_copy(ph, zz, x).start()

        mate_p(ph, zz, x, c).start()

    def x_stage(ph, k):
        zz = nearest(k)
        for dx in range(1, x_size):
            xx = (x + x_size - dx) % x_size
            plane_wait(ph, zz, xx)
            y_copy(ph, zz, xx).start()
            mate_p(ph, zz, xx, c).start()

    def y_stage(ph, k):
        zz = nearest(k)
        for dx in range(x_size):
            xx = (x + x_size - dx) % x_size
            if dx == 0:

                @pl.when(k > 0)
                def _():
                    y_wait(ph, zz, xx)

            else:
                y_wait(ph, zz, xx)
            mate_y(ph, zz, xx, c).start()

    def c_stage(ph, k):
        zz = nearest(k)
        for dx in range(x_size):
            xx = (x + x_size - dx) % x_size
            mate_p(ph, zz, xx, 1 - c).wait_recv()
            mate_y(ph, zz, xx, 1 - c).wait_recv()
            start = pl.multiple_of((zz * x_size + xx) * (2 * rows), 128)
            columns = vis[:, pl.ds(start, 2 * rows)]
            block = wbuf[ph, zz, xx].reshape(2 * rows, per)
            acc[ph] += jnp.dot(columns, block, preferred_element_type=jnp.float32)

    def first_small():
        small_wait(0, info_src, ibuf)
        small_wait(1, query_src, qbuf)
        for copy in later:
            copy.wait()
        pages = down_ref.shape[1]
        row = lax.broadcasted_iota(jnp.int32, (rank, pages), 0)
        column = lax.broadcasted_iota(jnp.int32, (rank, pages), 1)
        chosen = [
            (column == ibuf[d, 0:1, 0:1] * rank + row).astype(jnp.float32).astype(jnp.bfloat16)
            for d in range(n)
        ]
        picked = lax.dot_general(
            jnp.concatenate(chosen, axis=0),
            down_ref[...],
            (((1,), (1,)), ((), ())),
            preferred_element_type=jnp.float32,
        ).astype(jnp.bfloat16)
        selb[...] = picked.reshape(n, rank, rows)
        dbuf[me] = selb[me]
        small_start(2, sel_src, dbuf)

    def lowrank():
        small_wait(2, sel_src, dbuf)
        total = jnp.zeros((keys, rank), jnp.float32)
        for p in range(n // 2):
            pair = vis[:, p * 2 * rows : (p + 1) * 2 * rows]
            for half in range(2):
                total += lax.dot_general(
                    pair[:, half * rows : (half + 1) * rows],
                    dbuf[2 * p + half],
                    (((1,), (1,)), ((), ())),
                    preferred_element_type=jnp.float32,
                )
        low[...] = jnp.dot(
            total.astype(jnp.bfloat16), up_ref[page], preferred_element_type=jnp.float32
        )

    def usable():
        lane = lax.broadcasted_iota(jnp.int32, (1, lanes), 1) // group_of
        request = jnp.zeros((1, lanes), jnp.int32)
        for t in range(n):
            request = jnp.where(lane == t, ibuf[t, 1:2, 0:1], request)
        position = lax.broadcasted_iota(jnp.int32, (keys, lanes), 0)
        return jnp.logical_and(
            jnp.broadcast_to(request, (keys, lanes)) == owner,
            position < tiles_ref[0] * (keys // TILES),
        )

    def score():
        mask = usable()
        gain = gain_ref[...]
        for h in range(KV_HEADS):
            column = h % (KV_HEADS // SPLIT) * HEAD
            head = acc[h // (KV_HEADS // SPLIT), :, column : column + HEAD]
            scale = lax.rsqrt(jnp.mean(head * head, axis=-1, keepdims=True) + epsilon)
            block = (head * scale * gain).astype(jnp.bfloat16)
            query = qbuf[...].astype(jnp.float32)[:, h * group_of : (h + 1) * group_of, :]
            query = query.reshape(lanes, HEAD).astype(jnp.bfloat16)
            s = lax.dot_general(
                block, query, (((1,), (1,)), ((), ())), preferred_element_type=jnp.float32
            ) * HEAD ** (-0.5)
            s = jnp.where(mask, s, masked_score)
            sbuf[h] = s
            mbuf[me, h : h + 1, :] = jnp.max(s, axis=0, keepdims=True)
        small_start(3, max_src, mbuf)

    def weigh():
        small_wait(3, max_src, mbuf)
        mask = usable()
        top = jnp.max(mbuf[...], axis=0)
        for h in range(KV_HEADS):
            w = jnp.where(mask, jnp.exp(sbuf[h] - top[h : h + 1, :]), 0.0).astype(jnp.bfloat16)
            pbuf[h] = w
            lbuf[me, h : h + 1, :] = jnp.sum(w.astype(jnp.float32), axis=0, keepdims=True)
        small_start(4, total_src, lbuf)

    def divide():
        small_wait(4, total_src, lbuf)
        total = jnp.sum(lbuf[...], axis=0)
        for h in range(KV_HEADS):
            inv[h] = jnp.broadcast_to(total[h : h + 1, :], (HEAD, lanes)).T

    acc[...] = jnp.zeros_like(acc)
    mbuf[me] = jnp.zeros(mbuf.shape[1:], jnp.float32)
    lbuf[me] = jnp.zeros(lbuf.shape[1:], jnp.float32)
    small_start(0, info_src, ibuf)
    small_start(1, query_src, qbuf)

    steps = phases * z_size
    keys_done = SPLIT * z_size - 1 + LAG_C

    def step(t, carry):
        def at(lag, stage):
            now = t - lag

            @pl.when(jnp.logical_and(now >= 0, now < steps))
            def _():
                stage(now // z_size, now % z_size)

        at(0, z_stage)
        at(LAG_X, x_stage)
        at(LAG_Y, y_stage)

        @pl.when(t == 0)
        def _():
            first_small()

        at(LAG_C, c_stage)

        @pl.when(t == 2)
        def _():
            lowrank()

        @pl.when(t == keys_done)
        def _():
            score()

        @pl.when(t == keys_done + 1)
        def _():
            weigh()

        @pl.when(t == keys_done + 2)
        def _():
            divide()

        return carry

    lax.fori_loop(0, steps + LAG_C, step, 0)

    for h in range(KV_HEADS):
        column = h % (KV_HEADS // SPLIT) * HEAD
        value = acc[SPLIT + h // (KV_HEADS // SPLIT), :, column : column + HEAD]
        numerator = lax.dot_general(
            pbuf[h],
            (value + low[:, h * HEAD : (h + 1) * HEAD]).astype(jnp.bfloat16),
            (((0,), (0,)), ((), ())),
            preferred_element_type=jnp.float32,
        )
        share = numerator / inv[h]
        rbuf[:, h * group_of : (h + 1) * group_of, :] = share.reshape(n, group_of, HEAD)
    obuf[...] = rbuf[...].astype(jnp.bfloat16)
    qbuf[me] = obuf[me]
    small_start(5, num_src, qbuf)

    def drain(i, carry):
        ph, k = i // z_size, i % z_size
        zz = nearest(k)

        @pl.when(goes_up(zz))
        def _():
            z_copy(ph, zz, True).wait_send()

        @pl.when(goes_down(zz))
        def _():
            z_copy(ph, zz, False).wait_send()

        for dx in range(1, x_size):
            x_copy(ph, zz, dx).wait_send()
        for dx in range(x_size):
            xx = (x + x_size - dx) % x_size
            if dx == 0:

                @pl.when(k > 0)
                def _():
                    y_copy(ph, zz, xx).wait_send()

            else:
                y_copy(ph, zz, xx).wait_send()
            mate_p(ph, zz, xx, c).wait_send()
            mate_y(ph, zz, xx, c).wait_send()
        return carry

    lax.fori_loop(0, steps, drain, 0)
    small_wait(5, num_src, qbuf)
    qrows[...] = jnp.sum(qbuf[...].astype(jnp.float32), axis=0)
    for h in range(qrows.shape[0]):
        out_ref[:, h * HEAD : (h + 1) * HEAD] = qrows[h : h + 1, :].astype(jnp.bfloat16)


def local(
    n,
    vision,
    queries,
    text_request,
    key_weight,
    value_weight,
    key_gain,
    down_pages,
    up_pages,
    image_request,
    image_tiles,
    request_tenant,
    tenant_page,
):
    z_size, x_size = plane_of(n)
    rows, width = key_weight.shape
    keys, model = vision.shape[1:]
    rank = up_pages.shape[1]
    heads = queries.shape[1] // HEAD
    lanes = n * (heads // KV_HEADS)
    fy = rows * 3 // 8 // 16 * 16
    vmem = pl.BlockSpec(memory_space=pltpu.VMEM)
    hbm = pl.BlockSpec(memory_space=pltpu.HBM)
    dma = pltpu.SemaphoreType.DMA
    phases = 2 * SPLIT
    blocks = (phases, z_size, x_size)
    attended = pl.pallas_call(
        functools.partial(kernel, n, fy),
        out_shape=jax.ShapeDtypeStruct((1, heads * HEAD), jnp.bfloat16),
        in_specs=[hbm] * 12,
        out_specs=vmem,
        scratch_shapes=[
            pltpu.VMEM((1, HEAD), jnp.float32),
            pltpu.VMEM(down_pages.shape, jnp.bfloat16),
            pltpu.VMEM(up_pages.shape, jnp.bfloat16),
            pltpu.SMEM(text_request.shape, jnp.int32),
            pltpu.SMEM(image_request.shape, jnp.int32),
            pltpu.SMEM(image_tiles.shape, jnp.int32),
            pltpu.SMEM(request_tenant.shape, jnp.int32),
            pltpu.SMEM(tenant_page.shape, jnp.int32),
            pltpu.VMEM(queries.shape, jnp.bfloat16),
            pltpu.VMEM((heads, HEAD), jnp.float32),
            pltpu.VMEM((keys, model), jnp.bfloat16),
            pltpu.VMEM((phases, z_size, x_size, 2, rows, width // SPLIT), jnp.bfloat16),
            pltpu.VMEM((phases, keys, width // SPLIT), jnp.float32),
            pltpu.VMEM((n, heads, HEAD), jnp.bfloat16),
            pltpu.VMEM((n, 8, 128), jnp.int32),
            pltpu.VMEM((n, rank, rows), jnp.bfloat16),
            pltpu.VMEM((n, rank, rows), jnp.bfloat16),
            pltpu.VMEM((KV_HEADS, keys, lanes), jnp.float32),
            pltpu.VMEM((KV_HEADS, keys, lanes), jnp.bfloat16),
            pltpu.VMEM((n, 8, lanes), jnp.float32),
            pltpu.VMEM((n, 8, lanes), jnp.float32),
            pltpu.VMEM((keys, width), jnp.float32),
            pltpu.VMEM((KV_HEADS, lanes, HEAD), jnp.float32),
            pltpu.VMEM((n, heads, HEAD), jnp.bfloat16),
            pltpu.VMEM((n, heads, HEAD), jnp.float32),
            dma((10 + phases,)),
            dma((2, phases, z_size)),
            dma((max(x_size - 1, 1), phases, z_size)),
            dma(blocks),
            dma(blocks),
            dma(blocks),
            dma(blocks),
            dma(blocks),
            dma(blocks),
            dma(blocks),
            dma((6, n)),
            dma((6, n)),
        ],
        compiler_params=pltpu.CompilerParams(
            collective_id=0, has_side_effects=True, vmem_limit_bytes=60 * 1024 * 1024
        ),
    )(
        vision[0],
        queries,
        text_request,
        key_weight,
        value_weight,
        key_gain.reshape(1, HEAD),
        down_pages,
        up_pages,
        image_request,
        image_tiles,
        request_tenant,
        tenant_page,
    )
    return attended


def solution(mesh):
    in_specs = (
        P(("groups", "image"), None, None),
        P(("groups", "image"), None),
        P(("groups", "image")),
        P("image", None),
        P("image", None),
        P(),
        P("image", None),
        P(),
        P(("groups", "image"), None),
        P(("groups", "image")),
        P("groups"),
        P(),
    )
    out_specs = P(("groups", "image"), None)
    return jax.shard_map(
        functools.partial(local, mesh.shape["image"]),
        mesh=mesh,
        in_specs=in_specs,
        out_specs=out_specs,
        check_vma=False,
    )
```

```python
import functools

import jax
import jax.numpy as jnp
from jax import lax
from jax.experimental import pallas as pl
from jax.experimental.pallas import tpu as pltpu
from jax.sharding import PartitionSpec as P

HEAD = 128
KV_HEADS = 4
TILES = 4
MESH = pl.DeviceIdType.MESH

epsilon = 1e-05
masked_score = -1e30

LAG_X, LAG_Y, LAG_C = 1, 2, 3
SPLIT = 1


def plane_of(n):
    chips, x_size = n // 2, 1
    while (x_size * 2) ** 3 <= chips:
        x_size *= 2
    return chips // x_size, x_size


def kernel(
    n,
    fy,
    vision_hbm,
    query_hbm,
    text_hbm,
    key_hbm,
    value_hbm,
    gain_hbm,
    down_hbm,
    up_hbm,
    owner_hbm,
    tiles_hbm,
    tenant_hbm,
    page_hbm,
    out_ref,
    gain_ref,
    down_ref,
    up_ref,
    text_ref,
    owner_ref,
    tiles_ref,
    tenant_ref,
    page_ref,
    qrow,
    qrows,
    vis,
    wbuf,
    acc,
    qbuf,
    ibuf,
    selb,
    dbuf,
    sbuf,
    pbuf,
    mbuf,
    lbuf,
    low,
    inv,
    obuf,
    rbuf,
    local_sem,
    zs,
    xs,
    ys,
    mps,
    mys,
    plane_r,
    y_r,
    mp_r,
    my_r,
    small_s,
    small_r,
):
    z_size, x_size = plane_of(n)
    rows, width = key_hbm.shape
    rank = up_hbm.shape[1]
    keys = vision_hbm.shape[0]
    group_of = qbuf.shape[1] // KV_HEADS
    lanes = n * group_of
    g = lax.axis_index("groups")
    me = lax.axis_index("image")
    c = me % 2
    x = (me // 2) % x_size
    z = me // (2 * x_size)
    part = rows - fy
    p_rows = pl.ds(pl.multiple_of(g * fy, 16), part)
    y_rows = pl.ds(pl.multiple_of(g * part, 16), fy)
    o_rows = pl.ds(pl.multiple_of((1 - g) * part, 16), fy)

    def flat(zz, xx, cc):
        return (zz * x_size + xx) * 2 + cc

    phases = 2 * SPLIT
    per = width // SPLIT
    scalars = [
        pltpu.make_async_copy(src, dst, local_sem.at[i])
        for i, (src, dst) in enumerate(
            (
                (text_hbm, text_ref),
                (owner_hbm, owner_ref),
                (tiles_hbm, tiles_ref),
                (tenant_hbm, tenant_ref),
                (page_hbm, page_ref),
                (query_hbm, qrow),
            )
        )
    ]
    loads = [
        pltpu.make_async_copy(
            (key_hbm, value_hbm)[ph // SPLIT].at[:, pl.ds(ph % SPLIT * per, per)],
            wbuf.at[ph, z, x, c],
            local_sem.at[6 + ph],
        )
        for ph in range(phases)
    ]
    later = [
        pltpu.make_async_copy(src, dst, local_sem.at[6 + phases + i])
        for i, (src, dst) in enumerate(
            ((vision_hbm, vis), (gain_hbm, gain_ref), (down_hbm, down_ref), (up_hbm, up_ref))
        )
    ]
    for copy in scalars + loads + later:
        copy.start()

    barrier = pltpu.get_barrier_semaphore()

    def greet(d, carry):
        pl.semaphore_signal(barrier, inc=1, device_id=(g, (me + d) % n), device_id_type=MESH)
        return carry

    lax.fori_loop(1, n, greet, 0)
    pl.semaphore_signal(barrier, inc=1, device_id=(1 - g, me), device_id_type=MESH)
    for copy in scalars:
        copy.wait()
    owner = owner_ref[0, 0]
    page = page_ref[tenant_ref[owner]]
    ibuf[me] = jnp.where(
        lax.broadcasted_iota(jnp.int32, ibuf.shape[1:], 0) == 0, page, text_ref[0]
    )
    for h in range(qrows.shape[0]):
        qrows[h : h + 1, :] = qrow[:, h * HEAD : (h + 1) * HEAD].astype(jnp.float32)
    qbuf[me] = qrows[...].astype(jnp.bfloat16)
    for copy in loads:
        copy.wait()
    pl.semaphore_wait(barrier, n)

    def small(kind, src_of, dst, d):
        peer = (me + d) % n
        return pltpu.make_async_remote_copy(
            src_ref=src_of(peer),
            dst_ref=dst.at[me],
            send_sem=small_s.at[kind, d],
            recv_sem=small_r.at[kind, me],
            device_id=(g, peer),
            device_id_type=MESH,
        )

    def small_start(kind, src_of, dst):
        def body(d, carry):
            small(kind, src_of, dst, d).start()
            return carry

        lax.fori_loop(1, n, body, 0)

    def small_wait(kind, src_of, dst):
        def body(d, carry):
            source = (me + n - d) % n
            pltpu.make_async_remote_copy(
                src_ref=src_of(me),
                dst_ref=dst.at[source],
                send_sem=small_s.at[kind, d],
                recv_sem=small_r.at[kind, source],
                device_id=(g, source),
                device_id_type=MESH,
            ).wait_recv()
            small(kind, src_of, dst, d).wait_send()
            return carry

        lax.fori_loop(1, n, body, 0)

    def from_own(buffer):
        return lambda peer: buffer.at[me]

    info_src, query_src = from_own(ibuf), from_own(qbuf)
    max_src, total_src = from_own(mbuf), from_own(lbuf)

    def to_peer(buffer):
        return lambda peer: buffer.at[peer]

    sel_src, num_src = to_peer(selb), to_peer(obuf)

    def nearest(k):
        low_side = jnp.minimum(z, z_size - 1 - z)
        both = k <= 2 * low_side
        half = (k + 1) // 2
        rest = k - low_side
        paired = jnp.where(k % 2 == 1, z - half, z + half)
        single = jnp.where(z < z_size - 1 - z, z + rest, z - rest)
        return jnp.where(both, paired, single)

    def move(ph, zz, xx, cc, window, send, recv, device):
        ref = wbuf.at[ph, zz, xx, cc, window]
        return pltpu.make_async_remote_copy(
            src_ref=ref,
            dst_ref=ref,
            send_sem=send,
            recv_sem=recv,
            device_id=device,
            device_id_type=MESH,
        )

    def z_copy(ph, zz, up):
        to = z + 1 if up else z - 1
        return move(
            ph, zz, x, c, p_rows, zs.at[0 if up else 1, ph, zz],
            plane_r.at[ph, zz, x], (g, flat(to, x, c)),
        )

    def x_copy(ph, zz, dx):
        return move(
            ph, zz, x, c, p_rows, xs.at[dx - 1, ph, zz],
            plane_r.at[ph, zz, x], (g, flat(z, (x + dx) % x_size, c)),
        )

    def y_copy(ph, zz, xx):
        return move(
            ph, zz, xx, c, y_rows, ys.at[ph, zz, xx], y_r.at[ph, zz, xx], (1 - g, me)
        )

    def mate_p(ph, zz, xx, cc):
        return move(
            ph, zz, xx, cc, p_rows, mps.at[ph, zz, xx], mp_r.at[ph, zz, xx],
            (g, flat(z, x, 1 - c)),
        )

    def mate_y(ph, zz, xx, cc):
        return move(
            ph, zz, xx, cc, o_rows, mys.at[ph, zz, xx], my_r.at[ph, zz, xx],
            (g, flat(z, x, 1 - c)),
        )

    def plane_wait(ph, zz, xx):
        move(
            ph, zz, xx, c, p_rows, mps.at[ph, zz, xx], plane_r.at[ph, zz, xx],
            (g, flat(z, x, 1 - c)),
        ).wait_recv()

    def y_wait(ph, zz, xx):
        move(
            ph, zz, xx, c, o_rows, mys.at[ph, zz, xx], y_r.at[ph, zz, xx], (1 - g, me)
        ).wait_recv()

    def goes_up(zz):
        return jnp.logical_and(zz <= z, z + 1 < z_size)

    def goes_down(zz):
        return jnp.logical_and(zz >= z, z >= 1)

    def z_stage(ph, k):
        zz = nearest(k)

        @pl.when(k > 0)
        def _():
            plane_wait(ph, zz, x)

        @pl.when(goes_up(zz))
        def _():
            z_copy(ph, zz, True).start()

        @pl.when(goes_down(zz))
        def _():
            z_copy(ph, zz, False).start()

        for dx in range(1, x_size):
            x_copy(ph, zz, dx).start()

        @pl.when(k > 0)
        def _():
            y_copy(ph, zz, x).start()

        mate_p(ph, zz, x, c).start()

    def x_stage(ph, k):
        zz = nearest(k)
        for dx in range(1, x_size):
            xx = (x + x_size - dx) % x_size
            plane_wait(ph, zz, xx)
            y_copy(ph, zz, xx).start()
            mate_p(ph, zz, xx, c).start()

    def y_stage(ph, k):
        zz = nearest(k)
        for dx in range(x_size):
            xx = (x + x_size - dx) % x_size
            if dx == 0:

                @pl.when(k > 0)
                def _():
                    y_wait(ph, zz, xx)

            else:
                y_wait(ph, zz, xx)
            mate_y(ph, zz, xx, c).start()

    def c_stage(ph, k):
        zz = nearest(k)
        for dx in range(x_size):
            xx = (x + x_size - dx) % x_size
            mate_p(ph, zz, xx, 1 - c).wait_recv()
            mate_y(ph, zz, xx, 1 - c).wait_recv()
            start = pl.multiple_of((zz * x_size + xx) * (2 * rows), 128)
            columns = vis[:, pl.ds(start, 2 * rows)]
            block = wbuf[ph, zz, xx].reshape(2 * rows, per)
            acc[ph] += jnp.dot(columns, block, preferred_element_type=jnp.float32)

    def first_small():
        small_wait(0, info_src, ibuf)
        small_wait(1, query_src, qbuf)
        for copy in later:
            copy.wait()
        pages = down_ref.shape[1]
        row = lax.broadcasted_iota(jnp.int32, (rank, pages), 0)
        column = lax.broadcasted_iota(jnp.int32, (rank, pages), 1)
        chosen = [
            (column == ibuf[d, 0:1, 0:1] * rank + row).astype(jnp.float32).astype(jnp.bfloat16)
            for d in range(n)
        ]
        picked = lax.dot_general(
            jnp.concatenate(chosen, axis=0),
            down_ref[...],
            (((1,), (1,)), ((), ())),
            preferred_element_type=jnp.float32,
        ).astype(jnp.bfloat16)
        selb[...] = picked.reshape(n, rank, rows)
        dbuf[me] = selb[me]
        small_start(2, sel_src, dbuf)

    def lowrank():
        small_wait(2, sel_src, dbuf)
        total = jnp.zeros((keys, rank), jnp.float32)
        for p in range(n // 2):
            pair = vis[:, p * 2 * rows : (p + 1) * 2 * rows]
            for half in range(2):
                total += lax.dot_general(
                    pair[:, half * rows : (half + 1) * rows],
                    dbuf[2 * p + half],
                    (((1,), (1,)), ((), ())),
                    preferred_element_type=jnp.float32,
                )
        low[...] = jnp.dot(
            total.astype(jnp.bfloat16), up_ref[page], preferred_element_type=jnp.float32
        )

    def usable():
        lane = lax.broadcasted_iota(jnp.int32, (1, lanes), 1) // group_of
        request = jnp.zeros((1, lanes), jnp.int32)
        for t in range(n):
            request = jnp.where(lane == t, ibuf[t, 1:2, 0:1], request)
        position = lax.broadcasted_iota(jnp.int32, (keys, lanes), 0)
        return jnp.logical_and(
            jnp.broadcast_to(request, (keys, lanes)) == owner,
            position < tiles_ref[0] * (keys // TILES),
        )

    def score():
        mask = usable()
        gain = gain_ref[...]
        for h in range(KV_HEADS):
            column = h % (KV_HEADS // SPLIT) * HEAD
            head = acc[h // (KV_HEADS // SPLIT), :, column : column + HEAD]
            scale = lax.rsqrt(jnp.mean(head * head, axis=-1, keepdims=True) + epsilon)
            block = (head * scale * gain).astype(jnp.bfloat16)
            query = qbuf[...].astype(jnp.float32)[:, h * group_of : (h + 1) * group_of, :]
            query = query.reshape(lanes, HEAD).astype(jnp.bfloat16)
            s = lax.dot_general(
                block, query, (((1,), (1,)), ((), ())), preferred_element_type=jnp.float32
            ) * HEAD ** (-0.5)
            s = jnp.where(mask, s, masked_score)
            sbuf[h] = s
            mbuf[me, h : h + 1, :] = jnp.max(s, axis=0, keepdims=True)
        small_start(3, max_src, mbuf)

    def weigh():
        small_wait(3, max_src, mbuf)
        mask = usable()
        top = jnp.max(mbuf[...], axis=0)
        for h in range(KV_HEADS):
            w = jnp.where(mask, jnp.exp(sbuf[h] - top[h : h + 1, :]), 0.0).astype(jnp.bfloat16)
            pbuf[h] = w
            lbuf[me, h : h + 1, :] = jnp.sum(w.astype(jnp.float32), axis=0, keepdims=True)
        small_start(4, total_src, lbuf)

    def divide():
        small_wait(4, total_src, lbuf)
        total = jnp.sum(lbuf[...], axis=0)
        for h in range(KV_HEADS):
            inv[h] = jnp.broadcast_to(total[h : h + 1, :], (HEAD, lanes)).T

    acc[...] = jnp.zeros_like(acc)
    mbuf[me] = jnp.zeros(mbuf.shape[1:], jnp.float32)
    lbuf[me] = jnp.zeros(lbuf.shape[1:], jnp.float32)
    small_start(0, info_src, ibuf)
    small_start(1, query_src, qbuf)

    steps = phases * z_size
    keys_done = SPLIT * z_size - 1 + LAG_C

    def step(t, carry):
        def at(lag, stage):
            now = t - lag

            @pl.when(jnp.logical_and(now >= 0, now < steps))
            def _():
                stage(now // z_size, now % z_size)

        at(0, z_stage)
        at(LAG_X, x_stage)
        at(LAG_Y, y_stage)

        @pl.when(t == 0)
        def _():
            first_small()

        at(LAG_C, c_stage)

        @pl.when(t == 2)
        def _():
            lowrank()

        @pl.when(t == keys_done)
        def _():
            score()

        @pl.when(t == keys_done + 1)
        def _():
            weigh()

        @pl.when(t == keys_done + 2)
        def _():
            divide()

        return carry

    lax.fori_loop(0, steps + LAG_C, step, 0)

    for h in range(KV_HEADS):
        column = h % (KV_HEADS // SPLIT) * HEAD
        value = acc[SPLIT + h // (KV_HEADS // SPLIT), :, column : column + HEAD]
        numerator = lax.dot_general(
            pbuf[h],
            (value + low[:, h * HEAD : (h + 1) * HEAD]).astype(jnp.bfloat16),
            (((0,), (0,)), ((), ())),
            preferred_element_type=jnp.float32,
        )
        share = numerator / inv[h]
        rbuf[:, h * group_of : (h + 1) * group_of, :] = share.reshape(n, group_of, HEAD)
    obuf[...] = rbuf[...].astype(jnp.bfloat16)
    qbuf[me] = obuf[me]
    small_start(5, num_src, qbuf)

    def drain(i, carry):
        ph, k = i // z_size, i % z_size
        zz = nearest(k)

        @pl.when(goes_up(zz))
        def _():
            z_copy(ph, zz, True).wait_send()

        @pl.when(goes_down(zz))
        def _():
            z_copy(ph, zz, False).wait_send()

        for dx in range(1, x_size):
            x_copy(ph, zz, dx).wait_send()
        for dx in range(x_size):
            xx = (x + x_size - dx) % x_size
            if dx == 0:

                @pl.when(k > 0)
                def _():
                    y_copy(ph, zz, xx).wait_send()

            else:
                y_copy(ph, zz, xx).wait_send()
            mate_p(ph, zz, xx, c).wait_send()
            mate_y(ph, zz, xx, c).wait_send()
        return carry

    lax.fori_loop(0, steps, drain, 0)
    small_wait(5, num_src, qbuf)
    qrows[...] = jnp.sum(qbuf[...].astype(jnp.float32), axis=0)
    for h in range(qrows.shape[0]):
        out_ref[:, h * HEAD : (h + 1) * HEAD] = qrows[h : h + 1, :].astype(jnp.bfloat16)


def local(
    n,
    vision,
    queries,
    text_request,
    key_weight,
    value_weight,
    key_gain,
    down_pages,
    up_pages,
    image_request,
    image_tiles,
    request_tenant,
    tenant_page,
):
    z_size, x_size = plane_of(n)
    rows, width = key_weight.shape
    keys, model = vision.shape[1:]
    rank = up_pages.shape[1]
    heads = queries.shape[1] // HEAD
    lanes = n * (heads // KV_HEADS)
    fy = rows * 3 // 8 // 16 * 16
    vmem = pl.BlockSpec(memory_space=pltpu.VMEM)
    hbm = pl.BlockSpec(memory_space=pltpu.HBM)
    dma = pltpu.SemaphoreType.DMA
    phases = 2 * SPLIT
    blocks = (phases, z_size, x_size)
    attended = pl.pallas_call(
        functools.partial(kernel, n, fy),
        out_shape=jax.ShapeDtypeStruct((1, heads * HEAD), jnp.bfloat16),
        in_specs=[hbm] * 12,
        out_specs=vmem,
        scratch_shapes=[
            pltpu.VMEM((1, HEAD), jnp.float32),
            pltpu.VMEM(down_pages.shape, jnp.bfloat16),
            pltpu.VMEM(up_pages.shape, jnp.bfloat16),
            pltpu.SMEM(text_request.shape, jnp.int32),
            pltpu.SMEM(image_request.shape, jnp.int32),
            pltpu.SMEM(image_tiles.shape, jnp.int32),
            pltpu.SMEM(request_tenant.shape, jnp.int32),
            pltpu.SMEM(tenant_page.shape, jnp.int32),
            pltpu.VMEM(queries.shape, jnp.bfloat16),
            pltpu.VMEM((heads, HEAD), jnp.float32),
            pltpu.VMEM((keys, model), jnp.bfloat16),
            pltpu.VMEM((phases, z_size, x_size, 2, rows, width // SPLIT), jnp.bfloat16),
            pltpu.VMEM((phases, keys, width // SPLIT), jnp.float32),
            pltpu.VMEM((n, heads, HEAD), jnp.bfloat16),
            pltpu.VMEM((n, 8, 128), jnp.int32),
            pltpu.VMEM((n, rank, rows), jnp.bfloat16),
            pltpu.VMEM((n, rank, rows), jnp.bfloat16),
            pltpu.VMEM((KV_HEADS, keys, lanes), jnp.float32),
            pltpu.VMEM((KV_HEADS, keys, lanes), jnp.bfloat16),
            pltpu.VMEM((n, 8, lanes), jnp.float32),
            pltpu.VMEM((n, 8, lanes), jnp.float32),
            pltpu.VMEM((keys, width), jnp.float32),
            pltpu.VMEM((KV_HEADS, lanes, HEAD), jnp.float32),
            pltpu.VMEM((n, heads, HEAD), jnp.bfloat16),
            pltpu.VMEM((n, heads, HEAD), jnp.float32),
            dma((10 + phases,)),
            dma((2, phases, z_size)),
            dma((max(x_size - 1, 1), phases, z_size)),
            dma(blocks),
            dma(blocks),
            dma(blocks),
            dma(blocks),
            dma(blocks),
            dma(blocks),
            dma(blocks),
            dma((6, n)),
            dma((6, n)),
        ],
        compiler_params=pltpu.CompilerParams(
            collective_id=0, has_side_effects=True, vmem_limit_bytes=60 * 1024 * 1024
        ),
    )(
        vision[0],
        queries,
        text_request,
        key_weight,
        value_weight,
        key_gain.reshape(1, HEAD),
        down_pages,
        up_pages,
        image_request,
        image_tiles,
        request_tenant,
        tenant_page,
    )
    return attended


def solution(mesh):
    in_specs = (
        P(("groups", "image"), None, None),
        P(("groups", "image"), None),
        P(("groups", "image")),
        P("image", None),
        P("image", None),
        P(),
        P("image", None),
        P(),
        P(("groups", "image"), None),
        P(("groups", "image")),
        P("groups"),
        P(),
    )
    out_specs = P(("groups", "image"), None)
    return jax.shard_map(
        functools.partial(local, mesh.shape["image"]),
        mesh=mesh,
        in_specs=in_specs,
        out_specs=out_specs,
        check_vma=False,
    )
```
